32 devices in a mesh: dp: 2 (over x), row: 4 (over z), col: 4 (over y, core).
Axes of the slice: x: 2, y: 2, z: 4, core: 2. Of those that a mesh axis runs over, the one named last changes fastest.
Arguments:
- features: bfloat16 [2, 128, 128, 320], P('dp', 'row', 'col'), may hold values from -20 to 20
- norm1_gain: float32 [320], replicated, may hold values from 0.1 to 1.9
- conv1_kernel: bfloat16 [320, 9, 320], P('dp'), may hold values from -0.109375 to 0.109375
- norm2_gain: float32 [320], replicated, may hold values from 0.1 to 1.9
- conv2_kernel: bfloat16 [320, 9, 320], P('dp'), may hold values from -0.109375 to 0.109375
Outputs:
- block_out: bfloat16 [2, 128, 128, 320], P('dp', 'row', 'col')
The draws below stay inside these ranges and needn't reach their ends.
All inputs are finite; a program needn't handle non-finite values.
Results may differ from the reference program's by a relative error of at most 0.007.
Values may be sent and summed in bfloat16 or wider, within the bound.
No kernel may reach another device: no remote copies, remote signals or barrier semaphores. Data moves between devices by JAX's collectives and lax.ppermute only.
A program may use at most 64 MiB of HBM per device.

```python
import math
import jax
import jax.numpy as jnp
from jax import lax

C = 320
H = 128
W = 128
GROUPS = 32
BATCH = 2


def spread_regions(levels):
    levels = jnp.repeat(levels, H // 8, axis=1)
    levels = jnp.repeat(levels, W // 8, axis=2)
    return jnp.repeat(levels, C // GROUPS, axis=3)


def draw_features(key, part):
    key_base = jax.random.fold_in(key, 0)
    key_chan = jax.random.fold_in(key, 1)
    key_cell = jax.random.fold_in(key, 2)
    key_level = jax.random.fold_in(key, 4)
    key_offset = jax.random.fold_in(key, 5)
    base_draw = jnp.clip(jax.random.normal(key_base, (BATCH, H, W, C), jnp.float32), -4.0, 4.0)
    channel = jnp.exp(jax.random.uniform(key_chan, (C,), jnp.float32, 0.0, math.log(10.0))) / math.sqrt(10.0)
    cell_scale = jax.random.uniform(key_cell, (BATCH, H, W, 1), jnp.float32, 0.5, 1.5)
    row_index = jnp.arange(H, dtype=jnp.float32)[:, None]
    col_index = jnp.arange(W, dtype=jnp.float32)[None, :]
    ramp_scale = 0.5 + 1.5 * (row_index + col_index) / (H + W - 2)
    region_level = jnp.exp(jax.random.uniform(key_level, (BATCH, 8, 8, GROUPS), jnp.float32, -1.0, 1.0))
    region_offset = jax.random.uniform(key_offset, (BATCH, 8, 8, GROUPS), jnp.float32, -0.6, 0.6)
    values = 0.4 * base_draw * channel * cell_scale * ramp_scale[None, :, :, None] * spread_regions(region_level)
    values = values + spread_regions(region_offset)
    return jnp.clip(values, -20.0, 20.0).astype(jnp.bfloat16)


def level_of(own_key, dims, cuts, smallest, top_value):
    def one(dim, shards_of):
        steps = jax.random.uniform(jax.random.fold_in(jax.random.fold_in(own_key, 6), dim), (shards_of,), jnp.float32, smallest / len(cuts), top_value / len(cuts))
        return jnp.repeat(jnp.exp(steps), dims[dim] // shards_of).reshape((-1,) + (1,) * (len(dims) - dim - 1))

    level = one(*cuts[0])
    for cut in cuts[1:]:
        level = level * one(*cut)
    return level


def normal_values(rng, dims, width, most, cuts=(), kind=jnp.bfloat16):
    values = width * jax.random.normal(rng, dims, jnp.float32)
    if cuts:
        values = values * level_of(rng, dims, cuts, -0.22, 0.18)
    return jnp.clip(values, -most, most).astype(kind)


def setup_inputs(seed: int = 0) -> dict:
    key_of = jax.random.split(jax.random.key(seed), 6)
    return {
        "features": draw_features(jax.random.fold_in(key_of[5], 71), 0),
        "norm1_gain": jnp.clip(1.0 + 0.18 * jax.random.normal(key_of[1], (C,), jnp.float32), 0.1, 1.9),
        "conv1_kernel": normal_values(key_of[2], (C, 9, C), (9 * C) ** -0.5, 0.109375, ((0, 2),)),
        "norm2_gain": jnp.clip(1.0 + 0.18 * jax.random.normal(key_of[3], (C,), jnp.float32), 0.1, 1.9),
        "conv2_kernel": normal_values(key_of[4], (C, 9, C), (9 * C) ** -0.5, 0.109375, ((0, 2),)),
    }


EPS = 1e-05

def norm_silu(values, scale_gain):
    grouped = values.astype(jnp.float32).reshape(H * W, GROUPS, C // GROUPS)
    average = lax.optimization_barrier(jnp.mean(grouped, axis=(0, 2), keepdims=True))
    centred = grouped - average
    spread = lax.optimization_barrier(jnp.mean(centred * centred, axis=(0, 2), keepdims=True))
    normed = (centred * lax.rsqrt(spread + EPS)).reshape(H, W, C) * scale_gain.astype(jnp.float32)
    return jax.nn.silu(normed).astype(jnp.bfloat16)

def convolve(values, kernel):
    padded = jnp.pad(values, ((1, 1), (1, 1), (0, 0)))
    pieces = [padded[shift_row:shift_row + H, shift_col:shift_col + W, :] for shift_row in range(3) for shift_col in range(3)]
    stacked = jnp.concatenate(pieces, axis=-1).reshape(H * W, 9 * C)
    flat_kernel = kernel.reshape(C, 9 * C)
    result = lax.dot_general(stacked, flat_kernel, (((1,), (1,)), ((), ())), preferred_element_type=jnp.float32)
    return result.reshape(H, W, C)

def reference(features, norm1_gain, conv1_kernel, norm2_gain, conv2_kernel):

    def one_picture(picture):
        first_act = norm_silu(picture, norm1_gain)
        middle = convolve(first_act, conv1_kernel).astype(jnp.bfloat16)
        second_act = norm_silu(middle, norm2_gain)
        return (picture.astype(jnp.float32) + convolve(second_act, conv2_kernel)).astype(jnp.bfloat16)
    return lax.map(one_picture, features)
```

```python
import functools

import jax
import jax.numpy as jnp
from jax import lax
from jax.experimental import pallas as pl
from jax.experimental.pallas import tpu as pltpu
from jax.sharding import PartitionSpec as P

GROUPS = 32
EPS = 1e-05
ROWS = 16
F32 = jnp.float32
BF16 = jnp.bfloat16
MIB = 1 << 20


def split_rows(total, square):
    width = total.shape[1]
    at = lax.broadcasted_iota(jnp.int32, (ROWS, width), 0)
    out = jnp.zeros((ROWS, width), F32)
    for base, value in ((0, total), (3, square)):
        for step in range(3):
            part = value.astype(BF16).astype(F32)
            out = jnp.where(at == base + step, part, out)
            value = value - part
    return out.astype(BF16)


def join_rows(rows):
    return rows[0:1] + rows[1:2] + rows[2:3], rows[3:4] + rows[4:5] + rows[5:6]


def padded_lanes(width):
    return -(-3 * width // 128) * 128


def put_taps(store, taps, width):
    main = width // 128 * 128
    tail = width - main
    for e, tap in enumerate(taps):
        if main:
            store(e * main, main, tap[..., :main])
    if tail:
        for e, tap in enumerate(taps):
            store(3 * main + e * tail, tail, tap[..., main:])


def pack_body(kernel_ref, own_ref, send_ref, *, axis, parts):
    _, outs, width = kernel_ref.shape
    lanes = own_ref.shape[2]
    if 3 * width < lanes:
        own_ref[:, :, 3 * width :] = jnp.zeros((3, outs, lanes - 3 * width), BF16)
    for a in range(3):
        def store(at, size, value, a=a):
            own_ref[a, :, at : at + size] = value
        put_taps(store, [kernel_ref[3 * a + e] for e in range(3)], width)
    piece = outs // parts
    at = pl.multiple_of(lax.rem(lax.axis_index(axis), parts) * piece, ROWS)
    send_ref[...] = own_ref[:, pl.ds(at, piece), :]


def pack(kernel, axis, parts):
    outs, _, width = kernel.shape
    lanes = padded_lanes(width)
    return pl.pallas_call(
        functools.partial(pack_body, axis=axis, parts=parts),
        out_shape=(
            jax.ShapeDtypeStruct((3, outs, lanes), BF16),
            jax.ShapeDtypeStruct((3, outs // parts, lanes), BF16),
        ),
        compiler_params=pltpu.CompilerParams(vmem_limit_bytes=8 * MIB),
        name="pack",
    )(jnp.transpose(kernel, (1, 0, 2)))


def tile_stats(rows):
    return jnp.sum(rows, axis=0, keepdims=True), jnp.sum(rows * rows, axis=0, keepdims=True)


def put_messages(out_ref, rows, stats, up_ref, down_ref, own_ref):
    length, cells, width = out_ref.shape
    up_ref[:cells] = out_ref[length - 1]
    up_ref[cells:] = stats
    down_ref[:cells] = out_ref[0]
    down_ref[cells:] = stats
    own_ref[...] = stats


def first_body(tile_ref, up_ref, down_ref, own_ref):
    length, cells, width = tile_ref.shape
    total = jnp.zeros((1, width), F32)
    square = jnp.zeros((1, width), F32)
    step = 4
    for at in range(0, length, step):
        rows = tile_ref[at : at + step].reshape(step * cells, width).astype(F32)
        one, two = tile_stats(rows)
        total, square = total + one, square + two
    put_messages(tile_ref, None, split_rows(total, square), up_ref, down_ref, own_ref)


def message_shapes(cells, width):
    return (
        jax.ShapeDtypeStruct((cells + ROWS, width), BF16),
        jax.ShapeDtypeStruct((cells + ROWS, width), BF16),
        jax.ShapeDtypeStruct((ROWS, width), BF16),
    )


def first_messages(tile):
    length, cells, width = tile.shape
    return pl.pallas_call(
        first_body,
        out_shape=message_shapes(cells, width),
        compiler_params=pltpu.CompilerParams(vmem_limit_bytes=8 * MIB),
        name="first",
    )(tile)


def shifted(value, axis, by):
    size = lax.axis_size(axis)
    return lax.ppermute(value, axis, [(i, (i + by) % size) for i in range(size)])


def exchange(up, down, own, axis):
    size = lax.axis_size(axis)
    before = shifted(up, axis, 1)
    after = shifted(down, axis, size - 1)
    others = [shifted(own, axis, by) for by in range(2, size - 1)]
    return before, after, others


def summed(own_ref, before_ref, after_ref, other_refs, size):
    rows = own_ref[...].astype(F32)
    if size > 1:
        rows = rows + before_ref[before_ref.shape[0] - ROWS :].astype(F32)
    if size > 2:
        rows = rows + after_ref[after_ref.shape[0] - ROWS :].astype(F32)
    for other in other_refs:
        rows = rows + other[...].astype(F32)
    return join_rows(rows)


def edge_body(*refs, size, others):
    left_ref, right_ref, own_ref, before_ref, after_ref = refs[:5]
    other_refs = refs[5 : 5 + others]
    up_ref, down_ref, sum_ref = refs[5 + others :]
    length, width = left_ref.shape
    cells = before_ref.shape[0] - ROWS
    total, square = summed(own_ref, before_ref, after_ref, other_refs, size)
    stats = split_rows(total, square)
    sum_ref[...] = stats
    rows = up_ref.shape[0] - ROWS
    above = before_ref[:cells].astype(F32)
    below = after_ref[:cells].astype(F32)
    filler = jnp.zeros((rows - length - 2, width), F32)
    for out_ref, edge_ref, corner in ((up_ref, right_ref, cells - 1), (down_ref, left_ref, 0)):
        whole = [above[corner : corner + 1], edge_ref[...].astype(F32), below[corner : corner + 1], filler]
        out_ref[:rows] = jnp.concatenate(whole, axis=0).astype(BF16)
        out_ref[rows:] = stats


def edge_messages(left, right, own, before, after, others, size):
    length, width = left.shape
    rows = -(-(length + 2) // ROWS) * ROWS
    return pl.pallas_call(
        functools.partial(edge_body, size=size, others=len(others)),
        out_shape=message_shapes(rows, width),
        compiler_params=pltpu.CompilerParams(vmem_limit_bytes=8 * MIB),
        name="edge",
    )(left, right, own, before, after, *others)


def conv_body(*refs, pieces, others, size, count, skip, spread_axes, place):
    tile_ref, above_ref, below_ref, gain_ref, ones_ref, own_ref, left_ref, right_ref = refs[:8]
    at = 8
    other_refs = refs[at : at + others]
    at += others
    piece_refs = refs[at : at + pieces]
    at += pieces
    if skip:
        skip_ref = refs[at]
        at += 1
        out_ref = refs[at]
        at += 1
    else:
        out_ref, up_ref, down_ref, sum_ref = refs[at : at + 4]
        at += 4
    taps_ref, weight_ref, edge_ref, sems = refs[at:]

    length, cells, width = tile_ref.shape
    lanes = taps_ref.shape[2]
    copies = []
    for i, (piece, start) in enumerate(zip(piece_refs, place())):
        copy = pltpu.make_async_copy(
            piece, weight_ref.at[:, pl.ds(start, piece.shape[1]), :], sems.at[i]
        )
        copy.start()
        copies.append(copy)

    total, square = summed(own_ref, left_ref, right_ref, other_refs, size)
    grouped = jnp.dot(split_rows(total, square), ones_ref[...], preferred_element_type=F32)
    total, square = join_rows(grouped)
    average = total / count
    spread = jnp.maximum(square / count - average * average, 0.0)
    scale = lax.rsqrt(spread + EPS) * gain_ref[...]

    def act(value):
        normed = (value.astype(F32) - average) * scale
        return normed * (0.5 + 0.5 * jnp.tanh(0.5 * normed))

    row_axis, col_axis = spread_axes
    row, col = lax.axis_index(row_axis), lax.axis_index(col_axis)
    last_row, last_col = lax.axis_size(row_axis) - 1, lax.axis_size(col_axis) - 1
    rows = left_ref.shape[0] - ROWS
    edge_ref[0] = jnp.where(col > 0, act(left_ref[:rows]), 0.0)
    edge_ref[1] = jnp.where(col < last_col, act(right_ref[:rows]), 0.0)
    if 3 * width < lanes:
        taps_ref[:, :, 3 * width :] = jnp.zeros((length + 2, cells, lanes - 3 * width), BF16)
    where = lax.broadcasted_iota(jnp.int32, (cells, width), 0)

    def put_row(i, centre):
        left = jnp.where(where == 0, edge_ref[0, pl.ds(i, 1), :], pltpu.roll(centre, 1, 0))
        right = jnp.where(where == cells - 1, edge_ref[1, pl.ds(i, 1), :], pltpu.roll(centre, cells - 1, 0))

        def store(at, size, value):
            taps_ref[i, :, at : at + size] = value

        put_taps(store, [left.astype(BF16), centre.astype(BF16), right.astype(BF16)], width)

    def one_row(i, carry):
        put_row(i + 1, act(tile_ref[i]))
        return carry

    lax.fori_loop(0, length, one_row, 0, unroll=4)

    def border(i, source, inside):
        put_row(i, jnp.where(inside, act(source[:cells]), 0.0))
        for e in range(2):
            pass

    edge_ref[0, 0:1, :] = jnp.where(row > 0, edge_ref[0, 0:1, :], 0.0)
    edge_ref[1, 0:1, :] = jnp.where(row > 0, edge_ref[1, 0:1, :], 0.0)
    edge_ref[0, length + 1 : length + 2, :] = jnp.where(row < last_row, edge_ref[0, length + 1 : length + 2, :], 0.0)
    edge_ref[1, length + 1 : length + 2, :] = jnp.where(row < last_row, edge_ref[1, length + 1 : length + 2, :], 0.0)
    border(0, above_ref, row > 0)
    border(length + 1, below_ref, row < last_row)

    for copy in copies:
        copy.wait()

    outs = out_ref.shape[2]
    step = 8
    total = jnp.zeros((1, outs), F32)
    square = jnp.zeros((1, outs), F32)
    for start in range(0, length, step):
        result = None
        for a in range(3):
            part = lax.dot_general(
                taps_ref[start + a : start + a + step].reshape(step * cells, lanes),
                weight_ref[a],
                (((1,), (1,)), ((), ())),
                preferred_element_type=F32,
            )
            result = part if result is None else result + part
        if skip:
            result = result + skip_ref[start : start + step].reshape(step * cells, outs).astype(F32)
            out_ref[start : start + step] = result.astype(BF16).reshape(step, cells, outs)
        else:
            rounded = result.astype(BF16)
            out_ref[start : start + step] = rounded.reshape(step, cells, outs)
            one, two = tile_stats(rounded.astype(F32))
            total, square = total + one, square + two
    if not skip:
        put_messages(out_ref, None, split_rows(total, square), up_ref, down_ref, sum_ref)


def convolve(tile, above, below, gain, ones, own, left, right, others, pieces, place, count, skip):
    length, cells, width = tile.shape
    outs = width
    lanes = padded_lanes(width)
    rows = left.shape[0] - ROWS
    out = (jax.ShapeDtypeStruct((length, cells, outs), BF16),)
    if skip is None:
        out = out + message_shapes(cells, outs)
    vmem = pl.BlockSpec(memory_space=pltpu.VMEM)
    anywhere = pl.BlockSpec(memory_space=pl.ANY)
    skips = [] if skip is None else [skip]
    return pl.pallas_call(
        functools.partial(
            conv_body,
            pieces=len(pieces),
            others=len(others),
            size=lax.axis_size("col"),
            count=count,
            skip=skip is not None,
            spread_axes=("row", "col"),
            place=place,
        ),
        in_specs=[vmem] * (8 + len(others)) + [anywhere] * len(pieces) + [vmem] * len(skips),
        out_specs=(vmem,) * len(out),
        out_shape=out,
        scratch_shapes=[
            pltpu.VMEM((length + 2, cells, lanes), BF16),
            pltpu.VMEM((3, outs, lanes), BF16),
            pltpu.VMEM((2, rows, width), F32),
            pltpu.SemaphoreType.DMA((len(pieces),)),
        ],
        compiler_params=pltpu.CompilerParams(vmem_limit_bytes=24 * MIB),
        name="conv_skip" if skips else "conv",
    )(tile, above, below, gain, ones, own, left, right, *others, *pieces, *skips)


def gathered(kernel):
    outs = kernel.shape[0]
    size, cols = lax.axis_size("dp"), lax.axis_size("col")
    if size == 2 and cols % 2 == 0 and outs % (2 * ROWS) == 0:
        own, send = pack(kernel, "col", 2)
        got = lax.ppermute(send, "dp", [(0, 1), (1, 0)])
        mate = lax.ppermute(got, "col", [(i, i ^ 1) for i in range(cols)])
        piece = outs // 2

        def place():
            dp, half = lax.axis_index("dp"), lax.rem(lax.axis_index("col"), 2)
            other = (1 - dp) * outs
            return [
                pl.multiple_of(dp * outs, ROWS),
                pl.multiple_of(other + half * piece, ROWS),
                pl.multiple_of(other + (1 - half) * piece, ROWS),
            ]

        return [own, got, mate], place
    whole = lax.all_gather(kernel, "dp", axis=0, tiled=True)
    return [pack(whole, "col", 1)[0]], lambda: [0]


def normed_conv(tile, up, down, own, gain, ones, pieces, place, count, skip):
    above, below, others = exchange(up, down, own, "row")
    size = lax.axis_size("row")
    up, down, own = edge_messages(tile[:, 0], tile[:, -1], own, above, below, others, size)
    left, right, others = exchange(up, down, own, "col")
    return convolve(tile, above, below, gain, ones, own, left, right, others, pieces, place, count, skip)


def local(features, norm1_gain, conv1_kernel, norm2_gain, conv2_kernel):
    _, length, cells, width = features.shape
    members = width // GROUPS
    count = length * cells * lax.axis_size("row") * lax.axis_size("col") * members
    tile = features[0]
    group = jnp.arange(width) // members
    ones = (group[:, None] == group[None, :]).astype(BF16)
    pieces1, place1 = gathered(conv1_kernel)
    pieces2, place2 = gathered(conv2_kernel)
    up, down, own = first_messages(tile)
    middle, up, down, own = normed_conv(
        tile, up, down, own, norm1_gain[None], ones, pieces1, place1, count, None
    )
    (result,) = normed_conv(
        middle, up, down, own, norm2_gain[None], ones, pieces2, place2, count, tile
    )
    return result[None]


def solution(mesh):
    return jax.shard_map(
        local,
        mesh=mesh,
        in_specs=(P("dp", "row", "col", None), P(), P("dp", None, None), P(), P("dp", None, None)),
        out_specs=P("dp", "row", "col", None),
        check_vma=False,
    )
```

```python
import functools

import jax
import jax.numpy as jnp
from jax import lax
from jax.experimental import pallas as pl
from jax.experimental.pallas import tpu as pltpu
from jax.sharding import PartitionSpec as P


GROUPS = 32
EPS = 1e-05
ROWS = 16
F32 = jnp.float32
BF16 = jnp.bfloat16
MIB = 1 << 20


def split_rows(total, square):
    width = total.shape[1]
    at = lax.broadcasted_iota(jnp.int32, (ROWS, width), 0)
    out = jnp.zeros((ROWS, width), F32)
    for base, value in ((0, total), (3, square)):
        for step in range(3):
            part = value.astype(BF16).astype(F32)
            out = jnp.where(at == base + step, part, out)
            value = value - part
    return out.astype(BF16)


def join_rows(rows):
    return rows[0:1] + rows[1:2] + rows[2:3], rows[3:4] + rows[4:5] + rows[5:6]


def padded(size, to):
    return -(-size // to) * to


def padded_lanes(width):
    return padded(3 * width, 128)


def put_taps(store, taps, width):
    main = width // 128 * 128
    tail = width - main
    for e, tap in enumerate(taps):
        if main:
            store(e * main, main, tap[..., :main])
    if tail:
        for e, tap in enumerate(taps):
            store(3 * main + e * tail, tail, tap[..., main:])


def pack_body(kernel_ref, own_ref, send_ref, *, axis, parts):
    _, outs, width = kernel_ref.shape
    lanes = own_ref.shape[2]
    if 3 * width < lanes:
        own_ref[:, :, 3 * width :] = jnp.zeros((3, outs, lanes - 3 * width), BF16)
    for a in range(3):
        def store(at, size, value, a=a):
            own_ref[a, :, at : at + size] = value

        put_taps(store, [kernel_ref[3 * a + e] for e in range(3)], width)
    piece = outs // parts
    at = pl.multiple_of(lax.rem(lax.axis_index(axis), parts) * piece, ROWS)
    send_ref[...] = own_ref[:, pl.ds(at, piece), :]


def pack(kernel, axis, parts):
    outs, _, width = kernel.shape
    lanes = padded_lanes(width)
    return pl.pallas_call(
        functools.partial(pack_body, axis=axis, parts=parts),
        out_shape=(
            jax.ShapeDtypeStruct((3, outs, lanes), BF16),
            jax.ShapeDtypeStruct((3, outs // parts, lanes), BF16),
        ),
        compiler_params=pltpu.CompilerParams(vmem_limit_bytes=8 * MIB),
        name="pack",
    )(jnp.transpose(kernel, (1, 0, 2)))


def tile_stats(rows):
    return jnp.sum(rows, axis=0, keepdims=True), jnp.sum(rows * rows, axis=0, keepdims=True)


def carries(size, k):
    return any(abs(i - (i ^ k)) == 1 for i in range(size))


def faces_next(axis, k):
    me = lax.axis_index(axis)
    return (me ^ k) == me + 1


def faces_last(axis, k):
    me = lax.axis_index(axis)
    return (me ^ k) == me - 1


def put_messages(out_ref, stats, message_refs):
    length, cells, _ = out_ref.shape
    for i, ref in enumerate(message_refs):
        if ref.shape[0] > ROWS:
            ref[:cells] = out_ref[jnp.where(faces_next("row", i + 1), length - 1, 0)]
            ref[cells:] = stats
        else:
            ref[...] = stats


def first_body(tile_ref, *message_refs):
    length, cells, width = tile_ref.shape
    total = jnp.zeros((1, width), F32)
    square = jnp.zeros((1, width), F32)
    step = 4
    for at in range(0, length, step):
        rows = tile_ref[at : at + step].reshape(step * cells, width).astype(F32)
        one, two = tile_stats(rows)
        total, square = total + one, square + two
    put_messages(tile_ref, split_rows(total, square), message_refs)


def message_shapes(cells, width, axis):
    size = lax.axis_size(axis)
    rows = [cells + ROWS if carries(size, k) else ROWS for k in range(1, size)]
    return tuple(jax.ShapeDtypeStruct((n, width), BF16) for n in rows + [ROWS] * (size == 1))


def first_messages(tile):
    _, cells, width = tile.shape
    return pl.pallas_call(
        first_body,
        out_shape=message_shapes(cells, width, "row"),
        compiler_params=pltpu.CompilerParams(vmem_limit_bytes=8 * MIB),
        name="first",
    )(tile)


def exchange(messages, axis):
    size = lax.axis_size(axis)
    if size == 1:
        return list(messages)
    return [
        lax.ppermute(value, axis, [(i, i ^ (k + 1)) for i in range(size)])
        for k, value in enumerate(messages)
    ]


def summed(own, refs, size):
    rows = own.astype(F32)
    for ref in refs if size > 1 else ():
        rows = rows + ref[ref.shape[0] - ROWS :].astype(F32)
    return join_rows(rows)


def halos(refs, axis):
    before = after = None
    for i, ref in enumerate(refs):
        if ref.shape[0] > ROWS:
            value = ref[: ref.shape[0] - ROWS].astype(F32)
            before = value if before is None else jnp.where(faces_last(axis, i + 1), value, before)
            after = value if after is None else jnp.where(faces_next(axis, i + 1), value, after)
    return before, after


def edge_body(edge_ref, own_ref, *refs, size):
    got = max(size - 1, 1)
    row_refs, out_refs = refs[:got], refs[got:]
    _, length, width = edge_ref.shape
    own = own_ref[own_ref.shape[0] - ROWS :]
    total, square = summed(own, row_refs, size)
    stats = split_rows(total, square)
    above, below = halos(row_refs, "row")
    if above is None:
        above = below = jnp.zeros((1, width), F32)
    cells = above.shape[0]
    for i, ref in enumerate(out_refs):
        if ref.shape[0] > ROWS:
            rows = ref.shape[0] - ROWS
            right = faces_next("col", i + 1)
            top = jnp.where(right, above[cells - 1 : cells], above[0:1])
            bottom = jnp.where(right, below[cells - 1 : cells], below[0:1])
            filler = jnp.zeros((rows - length - 2, width), F32)
            middle = edge_ref[jnp.where(right, 1, 0)].astype(F32)
            ref[:rows] = jnp.concatenate([top, middle, bottom, filler], axis=0).astype(BF16)
            ref[rows:] = stats
        else:
            ref[...] = stats


def edge_messages(tile, own, got):
    length, _, width = tile.shape
    rows = padded(length + 2, ROWS)
    return pl.pallas_call(
        functools.partial(edge_body, size=lax.axis_size("row")),
        out_shape=message_shapes(rows, width, "col"),
        compiler_params=pltpu.CompilerParams(vmem_limit_bytes=8 * MIB),
        name="edge",
    )(jnp.stack([tile[:, 0], tile[:, -1]]), own, *got)


def conv_body(*refs, pieces, got, sizes, count, skip, place):
    tile_ref, gain_ref, ones_ref, own_ref = refs[:4]
    row_refs, col_refs = refs[4 : 4 + got[0]], refs[4 + got[0] : 4 + got[0] + got[1]]
    at = 4 + got[0] + got[1]
    piece_refs = refs[at : at + pieces]
    at += pieces
    if skip:
        skip_ref = refs[at]
        at += 1
    out_ref, message_refs = refs[at], refs[at + 1 : -4]
    taps_ref, weight_ref, edge_ref, sems = refs[-4:]

    length, cells, width = tile_ref.shape
    lanes = taps_ref.shape[2]
    copies = []
    for i, (piece, start) in enumerate(zip(piece_refs, place())):
        copy = pltpu.make_async_copy(
            piece, weight_ref.at[:, pl.ds(start, piece.shape[1]), :], sems.at[i]
        )
        copy.start()
        copies.append(copy)

    own = own_ref[own_ref.shape[0] - ROWS :]
    total, square = summed(own, col_refs, sizes[1])
    grouped = jnp.dot(split_rows(total, square), ones_ref[...], preferred_element_type=F32)
    total, square = join_rows(grouped)
    average = total / count
    spread = jnp.maximum(square / count - average * average, 0.0)
    scale = lax.rsqrt(spread + EPS) * gain_ref[...] * 0.5

    def act(value):
        half = (value.astype(F32) - average) * scale
        return half + half * jnp.tanh(half)

    row, col = lax.axis_index("row"), lax.axis_index("col")
    above, below = halos(row_refs, "row")
    left, right = halos(col_refs, "col")
    rows = edge_ref.shape[1]
    at = lax.broadcasted_iota(jnp.int32, (rows, width), 0)
    low = jnp.where(row > 0, 0, 1)
    high = jnp.where(row < sizes[0] - 1, length + 2, length + 1)
    held = (at >= low) & (at < high)
    for side, (edge, inside) in enumerate(((left, col > 0), (right, col < sizes[1] - 1))):
        if edge is None:
            edge_ref[side] = jnp.zeros((rows, width), F32)
        else:
            edge_ref[side] = jnp.where(held & inside, act(edge), 0.0)
    if 3 * width < lanes:
        taps_ref[:, :, 3 * width :] = jnp.zeros((length + 2, cells, lanes - 3 * width), BF16)
    where = lax.broadcasted_iota(jnp.int32, (cells, width), 0)

    def put_row(i, centre):
        left = jnp.where(where == 0, edge_ref[0, pl.ds(i, 1), :], pltpu.roll(centre, 1, 0))
        right = jnp.where(where == cells - 1, edge_ref[1, pl.ds(i, 1), :], pltpu.roll(centre, cells - 1, 0))

        def store(at, size, value):
            taps_ref[i, :, at : at + size] = value

        put_taps(store, [left.astype(BF16), centre.astype(BF16), right.astype(BF16)], width)

    def one_row(i, carry):
        put_row(i + 1, act(tile_ref[i]))
        return carry

    lax.fori_loop(0, length, one_row, 0, unroll=4)

    for i, source, inside in ((0, above, row > 0), (length + 1, below, row < sizes[0] - 1)):
        if source is None:
            put_row(i, jnp.zeros((cells, width), F32))
        else:
            put_row(i, jnp.where(inside, act(source), 0.0))

    for copy in copies:
        copy.wait()

    outs = out_ref.shape[2]
    step = 8
    total = jnp.zeros((1, outs), F32)
    square = jnp.zeros((1, outs), F32)
    for start in range(0, length, step):
        result = None
        for a in range(3):
            part = lax.dot_general(
                taps_ref[start + a : start + a + step].reshape(step * cells, lanes),
                weight_ref[a],
                (((1,), (1,)), ((), ())),
                preferred_element_type=F32,
            )
            result = part if result is None else result + part
        if skip:
            result = result + skip_ref[start : start + step].reshape(step * cells, outs).astype(F32)
            out_ref[start : start + step] = result.astype(BF16).reshape(step, cells, outs)
        else:
            rounded = result.astype(BF16)
            out_ref[start : start + step] = rounded.reshape(step, cells, outs)
            one, two = tile_stats(rounded.astype(F32))
            total, square = total + one, square + two
    if not skip:
        put_messages(out_ref, split_rows(total, square), message_refs)


def convolve(tile, gain, ones, own, row_got, col_got, pieces, place, count, skip):
    length, cells, width = tile.shape
    lanes = padded_lanes(width)
    out = (jax.ShapeDtypeStruct((length, cells, width), BF16),)
    if skip is None:
        out = out + message_shapes(cells, width, "row")
    vmem = pl.BlockSpec(memory_space=pltpu.VMEM)
    anywhere = pl.BlockSpec(memory_space=pl.ANY)
    skips = [] if skip is None else [skip]
    return pl.pallas_call(
        functools.partial(
            conv_body,
            pieces=len(pieces),
            got=(len(row_got), len(col_got)),
            sizes=(lax.axis_size("row"), lax.axis_size("col")),
            count=count,
            skip=skip is not None,
            place=place,
        ),
        in_specs=[vmem] * (4 + len(row_got) + len(col_got)) + [anywhere] * len(pieces) + [vmem] * len(skips),
        out_specs=(vmem,) * len(out),
        out_shape=out,
        scratch_shapes=[
            pltpu.VMEM((length + 2, cells, lanes), BF16),
            pltpu.VMEM((3, width, lanes), BF16),
            pltpu.VMEM((2, padded(length + 2, ROWS), width), F32),
            pltpu.SemaphoreType.DMA((len(pieces),)),
        ],
        compiler_params=pltpu.CompilerParams(vmem_limit_bytes=24 * MIB),
        name="conv_skip" if skips else "conv",
    )(tile, gain, ones, own, *row_got, *col_got, *pieces, *skips)


def gathered(kernel):
    outs = kernel.shape[0]
    cols = lax.axis_size("col")
    own, send = pack(kernel, "col", 2)

    def over(value):
        return lax.ppermute(value, "dp", [(0, 1), (1, 0)])

    def pair(value):
        return lax.ppermute(value, "col", [(i, i ^ 1) for i in range(cols)])

    piece = outs // 2

    def place():
        dp, half = lax.axis_index("dp"), lax.rem(lax.axis_index("col"), 2)
        other = (1 - dp) * outs
        return [
            pl.multiple_of(dp * outs, ROWS),
            pl.multiple_of(other + half * piece, ROWS),
            pl.multiple_of(other + (1 - half) * piece, ROWS),
        ]

    return own, send, over, pair, place


def whole_kernel(kernel):
    return pack(lax.all_gather(kernel, "dp", axis=0, tiled=True), "col", 1)[0]


def local(features, norm1_gain, conv1_kernel, norm2_gain, conv2_kernel):
    _, length, cells, width = features.shape
    members = width // GROUPS
    count = length * cells * lax.axis_size("row") * lax.axis_size("col") * members
    tile = features[0]
    group = jnp.arange(width) // members
    ones = (group[:, None] == group[None, :]).astype(BF16)
    split = lax.axis_size("dp") == 2 and lax.axis_size("col") % 2 == 0 and conv1_kernel.shape[0] % (2 * ROWS) == 0

    if split:
        own1, send1, over, pair, place = gathered(conv1_kernel)
        own2, send2 = gathered(conv2_kernel)[:2]
        got1 = over(send1)
        pieces1 = [own1, got1, pair(got1)]
        got2 = over(send2)
        pieces2 = [own2, got2, pair(got2)]
    else:
        pieces1, pieces2 = [whole_kernel(conv1_kernel)], [whole_kernel(conv2_kernel)]
        place = lambda: [0]

    messages = first_messages(tile)
    row_got = exchange(messages, "row")
    messages = edge_messages(tile, messages[-1], row_got)
    col_got = exchange(messages, "col")
    middle, *again = convolve(
        tile, norm1_gain[None], ones, messages[-1], row_got, col_got, pieces1, place, count, None
    )
    row_got = exchange(again, "row")
    messages = edge_messages(middle, again[-1], row_got)
    col_got = exchange(messages, "col")
    (result,) = convolve(
        middle, norm2_gain[None], ones, messages[-1], row_got, col_got, pieces2, place, count, tile
    )
    return result[None]


def solution(mesh):
    return jax.shard_map(
        local,
        mesh=mesh,
        in_specs=(P("dp", "row", "col", None), P(), P("dp", None, None), P(), P("dp", None, None)),
        out_specs=P("dp", "row", "col", None),
        check_vma=False,
    )
```
